32 devices in a mesh: chan: 2 (over x), row: 4 (over z), col: 4 (over y, core).
Axes of the slice: x: 2, y: 2, z: 4, core: 2. Of those that a mesh axis runs over, the one named last changes fastest.
Arguments:
- voltages: bfloat16 [2, 1024, 131072], P(None, 'chan', ('row', 'col')), may hold values from -6 to 6
- input_flags: int32 [1024], P('chan'), may hold values 0 or 1
- channel_order: int32 [128], replicated, may hold values from 0 to 127, each once
- beam_weights: bfloat16 [2, 128, 256, 1024], P(None, 'chan', 'col'), may hold values from -0.1875 to 0.1875
Outputs:
- visibility: float32 [2, 128, 1024, 1024], P(None, 'chan', 'row', 'col')
- beam_power: float32 [128, 256, 128], P('chan', 'col', 'row')
The draws below stay inside these ranges and needn't reach their ends.
Inputs may be any that keep to these rules, and one draw needn't show every extreme that they name: `channel_order`: every fine channel appears exactly once.
All inputs are finite; a program needn't handle non-finite values. No bound on the sum of `input_flags` on one device may be relied on, other than what follows from the above.
Results may differ from the reference program's by a relative error of at most 0.005.
Values may be sent and summed in bfloat16 or wider, within the bound.
A program may use at most 448 MiB of HBM per device.

```python
import math
import jax
import jax.numpy as jnp
from jax import lax

INPUTS = 1024
NCH = 128
TAPS = 4
BEAMS = 256
INTEG = 8
FRAMES = 1024
BINS = 128


def touch_ends(result, own_key, low, largest):
    index_at = [jax.random.randint(jax.random.fold_in(own_key, axis), (), 0, length) for axis, length in enumerate(result.shape)]
    widest = result.shape.index(max(result.shape))
    neighbour = index_at[:widest] + [(index_at[widest] + 1) % result.shape[widest]] + index_at[widest + 1:]
    return result.at[tuple(index_at)].set(low).at[tuple(neighbour)].set(largest)


def levels(stream_key, shape, pieces, least, largest):
    loudness = 1.0
    for dim, parts in pieces:
        draws = jax.random.uniform(jax.random.fold_in(jax.random.fold_in(stream_key, 6), dim), (parts,), jnp.float32, least / len(pieces), largest / len(pieces))
        loudness = loudness * jnp.repeat(jnp.exp(draws), shape[dim] // parts).reshape((-1,) + (1,) * (len(shape) - 1 - dim))
    return loudness


def normal_values(key, dims, spread, most, pieces=(), kind=jnp.bfloat16):
    level = levels(key, dims, pieces, -0.22, 0.18) if pieces else 1.0
    drawn = jax.random.normal(key, dims, jnp.float32) * spread * level
    return jnp.minimum(jnp.maximum(drawn, -most), most).astype(kind)


def setup_inputs(seed: int = 0) -> dict:
    seeds = jax.random.split(jax.random.key(seed), 5)
    voltages = normal_values(seeds[0], (2, INPUTS, FRAMES * NCH), 1.0, 6.0, ((1, 2), (2, 16)))
    input_flags = touch_ends((jax.random.randint(seeds[1], (INPUTS,), 0, 8) < 7).astype(jnp.int32), jax.random.fold_in(seeds[1], 1), 0, 1)
    channel_order = jax.random.permutation(seeds[2], NCH).astype(jnp.int32)
    beam_weights = normal_values(seeds[3], (2, NCH, BEAMS, INPUTS), INPUTS ** -0.5, 0.1875, ((1, 2), (2, 4)))
    return {"voltages": voltages, "input_flags": input_flags, "channel_order": channel_order, "beam_weights": beam_weights}


def prototype(taps, length):
    position = jnp.arange(taps * length, dtype=jnp.float32) + 0.5
    offset = position / length - taps / 2.0
    window = 0.5 - 0.5 * jnp.cos(2.0 * math.pi * position / (taps * length))
    return (jnp.sin(math.pi * offset) / (math.pi * offset) * window).reshape(taps, length)

def dft_tables(channel_rows, length):
    sample_index = jnp.arange(length, dtype=jnp.int32)
    product = channel_rows[:, None] * sample_index[None, :] % length
    angle = 2.0 * math.pi / length * product.astype(jnp.float32)
    factor = 1.0 / math.sqrt(length)
    cosine = jnp.cos(angle) * factor
    sine = jnp.sin(angle) * factor
    real_rows = jnp.stack([cosine, sine], axis=1)
    imag_rows = jnp.stack([-sine, cosine], axis=1)
    return jnp.stack([real_rows, imag_rows], axis=1).astype(jnp.bfloat16)

def reference(voltages, input_flags, channel_order, beam_weights):
    masked = voltages * input_flags.astype(jnp.bfloat16)[None, :, None]
    padded = jnp.concatenate([jnp.zeros((2, INPUTS, (TAPS - 1) * NCH), jnp.bfloat16), masked], axis=2)
    blocks = padded.reshape(2, INPUTS, FRAMES + TAPS - 1, NCH)
    coeffs = prototype(TAPS, NCH)
    filtered = jnp.zeros((2, INPUTS, FRAMES, NCH), jnp.float32)
    for tap_index in range(TAPS):
        filtered = filtered + coeffs[tap_index] * blocks[:, :, tap_index:tap_index + FRAMES].astype(jnp.float32)
    filtered = filtered.astype(jnp.bfloat16)
    tables = dft_tables(jnp.arange(NCH, dtype=jnp.int32), NCH)
    spectrum = jnp.einsum('kqpn,pifn->kiqf', tables.astype(jnp.float32), filtered.astype(jnp.float32), precision=lax.Precision.HIGHEST).astype(jnp.bfloat16)
    ordered = spectrum[channel_order]
    weights_by_channel = jnp.transpose(beam_weights, (1, 0, 2, 3))

    def per_channel(items):
        block, weights = items
        real_part = block[:, 0].astype(jnp.float32)
        imag_part = block[:, 1].astype(jnp.float32)
        vis_re = (jnp.dot(real_part, real_part.T, precision=lax.Precision.HIGHEST) + jnp.dot(imag_part, imag_part.T, precision=lax.Precision.HIGHEST)) / FRAMES
        vis_im = (jnp.dot(imag_part, real_part.T, precision=lax.Precision.HIGHEST) - jnp.dot(real_part, imag_part.T, precision=lax.Precision.HIGHEST)) / FRAMES
        w_real = weights[0].astype(jnp.float32)
        w_imag = weights[1].astype(jnp.float32)
        beam_re = jnp.dot(w_real, real_part, precision=lax.Precision.HIGHEST) - jnp.dot(w_imag, imag_part, precision=lax.Precision.HIGHEST)
        beam_im = jnp.dot(w_real, imag_part, precision=lax.Precision.HIGHEST) + jnp.dot(w_imag, real_part, precision=lax.Precision.HIGHEST)
        power = beam_re * beam_re + beam_im * beam_im
        binned = power.reshape(BEAMS, BINS, INTEG).mean(axis=-1)
        return (jnp.stack([vis_re, vis_im]), binned)
    vis_all, beam_power = lax.map(per_channel, (ordered, weights_by_channel))
    visibility = jnp.transpose(vis_all, (1, 0, 2, 3))
    return (visibility, beam_power)
```

```python
import functools
import math

import jax
import jax.numpy as jnp
from jax import lax
from jax.experimental import pallas as pl
from jax.experimental.pallas import tpu as pltpu
from jax.sharding import PartitionSpec as P

NCH = 128
TAPS = 4
INTEG = 8


def passed_along(value, axis, steps):
    count = lax.axis_size(axis)
    initial, last = (max(0, -steps), min(count, count - steps))
    return lax.ppermute(value, axis, [(source, source + steps) for source in range(initial, last)])


def prototype(taps, length):
    position = jnp.arange(taps * length, dtype=jnp.float32) + 0.5
    offset = position / length - taps / 2.0
    window = 0.5 - 0.5 * jnp.cos(2.0 * math.pi * position / (taps * length))
    return (jnp.sin(math.pi * offset) / (math.pi * offset) * window).reshape(taps, length)


def dft_tables(channel_rows, length):
    sample_index = jnp.arange(length, dtype=jnp.int32)
    product = channel_rows[:, None] * sample_index[None, :] % length
    angle = 2.0 * math.pi / length * product.astype(jnp.float32)
    factor = 1.0 / math.sqrt(length)
    cosine = jnp.cos(angle) * factor
    sine = jnp.sin(angle) * factor
    real_rows = jnp.stack([cosine, sine], axis=1)
    imag_rows = jnp.stack([-sine, cosine], axis=1)
    return jnp.stack([real_rows, imag_rows], axis=1).astype(jnp.bfloat16)


def to_frames(gathered, frames, outer, inner, swapped):
    chans = gathered.shape[0]
    width = gathered.shape[1]
    split = gathered.reshape(chans, width, outer, inner, 2, frames)
    if swapped:
        order = jnp.transpose(split, (0, 4, 1, 3, 2, 5))
    else:
        order = jnp.transpose(split, (0, 4, 1, 2, 3, 5))
    return order.reshape(chans, 2, width, outer * inner * frames)


def correlate_one(left_block, right_block, frame_count):
    left_re = left_block[0]
    left_im = left_block[1]
    right_re = right_block[0]
    right_im = right_block[1]
    dims = (((1,), (1,)), ((), ()))
    vis_re = lax.dot_general(left_re, right_re, dims, preferred_element_type=jnp.float32)
    vis_re = vis_re + lax.dot_general(left_im, right_im, dims, preferred_element_type=jnp.float32)
    vis_im = lax.dot_general(left_im, right_re, dims, preferred_element_type=jnp.float32)
    vis_im = vis_im - lax.dot_general(left_re, right_im, dims, preferred_element_type=jnp.float32)
    return jnp.stack([vis_re, vis_im]) / frame_count


def correlate(left_view, right_view, frame_count):
    result = lax.map(
        lambda items: correlate_one(items[0], items[1], frame_count), (left_view, right_view)
    )
    return jnp.transpose(result, (1, 0, 2, 3))


def beams_one(weights, block):
    w_real = weights[0]
    w_imag = weights[1]
    x_real = block[0]
    x_imag = block[1]
    beam_re = jnp.dot(w_real, x_real, preferred_element_type=jnp.float32) - jnp.dot(
        w_imag, x_imag, preferred_element_type=jnp.float32
    )
    beam_im = jnp.dot(w_real, x_imag, preferred_element_type=jnp.float32) + jnp.dot(
        w_imag, x_real, preferred_element_type=jnp.float32
    )
    return jnp.stack([beam_re, beam_im], axis=1)


def form_beams(weights, view):
    by_channel = jnp.transpose(weights, (1, 0, 2, 3))
    return lax.map(lambda items: beams_one(items[0], items[1]), (by_channel, view))


def integrate(voltage):
    power = voltage[:, :, 0] * voltage[:, :, 0] + voltage[:, :, 1] * voltage[:, :, 1]
    return power.reshape(power.shape[0], power.shape[1], -1, INTEG).mean(axis=-1)


def channelize(voltages, input_flags, channel_order):
    masked = voltages * input_flags.astype(jnp.bfloat16)[None, :, None]
    local_inputs = masked.shape[1]
    frames = masked.shape[2] // NCH
    history = passed_along(masked[:, :, masked.shape[2] - (TAPS - 1) * NCH :], ("row", "col"), 1)
    joined = jnp.concatenate([history, masked], axis=2)
    blocks = joined.reshape(2, local_inputs, frames + TAPS - 1, NCH)
    coeffs = prototype(TAPS, NCH)
    filtered = jnp.zeros((2, local_inputs, frames, NCH), jnp.float32)
    for tap_index in range(TAPS):
        filtered = filtered + coeffs[tap_index] * blocks[
            :, :, tap_index : tap_index + frames
        ].astype(jnp.float32)
    filtered = filtered.astype(jnp.bfloat16)
    tables = dft_tables(channel_order, NCH)
    spectrum = jnp.einsum(
        "kqpn,pifn->kiqf",
        tables.astype(jnp.float32),
        filtered.astype(jnp.float32),
        precision=lax.Precision.HIGHEST,
    ).astype(jnp.bfloat16)
    spectrum = spectrum.reshape(NCH, local_inputs, 2 * frames)
    return spectrum


def by_panels(voltages, input_flags, channel_order, beam_weights):
    spectrum = channelize(voltages, input_flags, channel_order)
    frames = spectrum.shape[2] // 2
    turned = lax.all_to_all(spectrum, "chan", split_axis=0, concat_axis=1, tiled=True)
    row_count = lax.axis_size("row")
    col_count = lax.axis_size("col")
    total_frames = frames * row_count * col_count
    row_turned = lax.all_to_all(turned, "row", split_axis=1, concat_axis=2, tiled=True)
    row_all = lax.all_gather(row_turned, "col", axis=2, tiled=True)
    col_turned = lax.all_to_all(turned, "col", split_axis=1, concat_axis=2, tiled=True)
    col_all = lax.all_gather(col_turned, "row", axis=2, tiled=True)
    row_view = to_frames(row_all, frames, col_count, row_count, True)
    col_view = to_frames(col_all, frames, row_count, col_count, False)
    visibility = correlate(row_view, col_view, total_frames)
    weights_all = lax.all_gather(beam_weights, "col", axis=2, tiled=True)
    local_view = to_frames(turned, frames, 1, 1, False)
    voltage = form_beams(weights_all, local_view)
    own_power = integrate(voltage)
    beam_power = lax.all_to_all(own_power, "col", split_axis=1, concat_axis=2, tiled=True)
    return (visibility, beam_power)


MESH = pl.DeviceIdType.MESH


def sizes():
    return lax.axis_size("chan"), lax.axis_size("row"), lax.axis_size("col")


def turn_kernel(cs, rs, qs, spec_ref, weight_ref, x_ref, w_ref, send, recv, wsend, wrecv, local):
    c, r, q = (lax.axis_index(name) for name in ("chan", "row", "col"))
    cells = rs * qs
    devices = cs * cells
    me = r * qs + q
    here = c * cells + me
    own = spec_ref.shape[0] // devices
    inputs = spec_ref.shape[1]
    lanes = spec_ref.shape[2]
    beams = weight_ref.shape[2]

    def place(chan, cell):
        return x_ref.at[
            :,
            pl.ds(pl.multiple_of(chan * inputs, inputs), inputs),
            pl.ds(pl.multiple_of(cell * lanes, lanes), lanes),
        ]

    def spectra(step, outgoing):
        if outgoing:
            chan, cell = (c + step % cs) % cs, (me + step // cs) % cells
            target = place(c, me)
            slot = here
        else:
            chan, cell = (c + cs - step % cs) % cs, (me + cells - step // cs) % cells
            target = place(chan, cell)
            slot = chan * cells + cell
        return pltpu.make_async_remote_copy(
            src_ref=spec_ref.at[pl.ds((chan * cells + cell) * own, own)],
            dst_ref=target,
            send_sem=send.at[chan * cells + cell],
            recv_sem=recv.at[slot],
            device_id=(chan, cell // qs, cell % qs),
            device_id_type=MESH,
        )

    def weights(step, outgoing):
        if outgoing:
            peer = (q + step) % qs
            slot = q
        else:
            peer = (q + qs - step) % qs
            slot = peer
        return pltpu.make_async_remote_copy(
            src_ref=weight_ref.at[:, pl.ds((r * qs + peer) * own, own)],
            dst_ref=w_ref.at[:, :, pl.ds(pl.multiple_of(slot * beams, beams), beams)],
            send_sem=wsend.at[peer],
            recv_sem=wrecv.at[slot],
            device_id=(c, r, peer),
            device_id_type=MESH,
        )

    def start(step, carry):
        spectra(step, True).start()
        return carry

    def start_weights(step, carry):
        weights(step, True).start()
        return carry

    lax.fori_loop(1, devices, start, 0)
    lax.fori_loop(1, qs, start_weights, 0)
    stay = pltpu.make_async_copy(spec_ref.at[pl.ds(here * own, own)], place(c, me), local.at[0])
    keep = pltpu.make_async_copy(
        weight_ref.at[:, pl.ds(me * own, own)],
        w_ref.at[:, :, pl.ds(pl.multiple_of(q * beams, beams), beams)],
        local.at[1],
    )
    stay.start()
    keep.start()

    def finish(step, carry):
        spectra(step, True).wait_send()
        spectra(step, False).wait_recv()
        return carry

    def finish_weights(step, carry):
        weights(step, True).wait_send()
        weights(step, False).wait_recv()
        return carry

    lax.fori_loop(1, devices, finish, 0)
    lax.fori_loop(1, qs, finish_weights, 0)
    stay.wait()
    keep.wait()


def turn(spectrum, beam_weights):
    cs, rs, qs = sizes()
    devices = cs * rs * qs
    own = spectrum.shape[0] // devices
    anywhere = pl.BlockSpec(memory_space=pl.ANY)
    return pl.pallas_call(
        functools.partial(turn_kernel, cs, rs, qs),
        out_shape=(
            jax.ShapeDtypeStruct(
                (own, spectrum.shape[1] * cs, spectrum.shape[2] * rs * qs), spectrum.dtype
            ),
            jax.ShapeDtypeStruct(
                (2, own, beam_weights.shape[2] * qs, beam_weights.shape[3]), beam_weights.dtype
            ),
        ),
        in_specs=[anywhere] * 2,
        out_specs=(anywhere,) * 2,
        scratch_shapes=[
            pltpu.SemaphoreType.DMA((devices,)),
            pltpu.SemaphoreType.DMA((devices,)),
            pltpu.SemaphoreType.DMA((qs,)),
            pltpu.SemaphoreType.DMA((qs,)),
            pltpu.SemaphoreType.DMA((2,)),
        ],
        compiler_params=pltpu.CompilerParams(has_side_effects=True),
        name="turn",
    )(spectrum, beam_weights)


def deliver_kernel(rs, qs, vis_ref, power_ref, block_ref, part_ref, send, recv, psend, precv, local):
    c, r, q = (lax.axis_index(name) for name in ("chan", "row", "col"))
    cells = rs * qs
    me = r * qs + q
    own, height, width = vis_ref.shape[1], block_ref.shape[2], block_ref.shape[3]

    def piece(row, col):
        return vis_ref.at[
            :,
            :,
            pl.ds(pl.multiple_of(row * height, height), height),
            pl.ds(pl.multiple_of(col * width, width), width),
        ]

    def copies(step, outgoing):
        if outgoing:
            cell = (me + step) % cells
            slot = me
        else:
            cell = (me + cells - step) % cells
            slot = cell
        device = (c, cell // qs, cell % qs)
        block = pltpu.make_async_remote_copy(
            src_ref=piece(cell // qs, cell % qs),
            dst_ref=block_ref.at[:, pl.ds(slot * own, own)],
            send_sem=send.at[cell],
            recv_sem=recv.at[slot],
            device_id=device,
            device_id_type=MESH,
        )
        part = pltpu.make_async_remote_copy(
            src_ref=power_ref.at[cell],
            dst_ref=part_ref.at[slot],
            send_sem=psend.at[cell],
            recv_sem=precv.at[slot],
            device_id=device,
            device_id_type=MESH,
        )
        return block, part

    def start(step, carry):
        for copy in copies(step, True):
            copy.start()
        return carry

    lax.fori_loop(1, cells, start, 0)
    stay = pltpu.make_async_copy(piece(r, q), block_ref.at[:, pl.ds(me * own, own)], local.at[0])
    keep = pltpu.make_async_copy(power_ref.at[me], part_ref.at[me], local.at[1])
    stay.start()
    keep.start()

    def finish(step, carry):
        for copy in copies(step, True):
            copy.wait_send()
        for copy in copies(step, False):
            copy.wait_recv()
        return carry

    lax.fori_loop(1, cells, finish, 0)
    stay.wait()
    keep.wait()


def deliver(visibility, power):
    _, rs, qs = sizes()
    cells = rs * qs
    own = visibility.shape[1]
    anywhere = pl.BlockSpec(memory_space=pl.ANY)
    return pl.pallas_call(
        functools.partial(deliver_kernel, rs, qs),
        out_shape=(
            jax.ShapeDtypeStruct(
                (2, own * cells, visibility.shape[2] // rs, visibility.shape[3] // qs),
                visibility.dtype,
            ),
            jax.ShapeDtypeStruct(power.shape, power.dtype),
        ),
        in_specs=[anywhere] * 2,
        out_specs=(anywhere,) * 2,
        scratch_shapes=[pltpu.SemaphoreType.DMA((cells,))] * 4 + [pltpu.SemaphoreType.DMA((2,))],
        compiler_params=pltpu.CompilerParams(has_side_effects=True),
        name="deliver",
    )(visibility, power)


def products_kernel(frame_count, tile, x_ref, w_ref, swap_ref, pool_ref, vis_ref, power_ref, y_ref):
    inputs, depth = x_ref.shape[1], x_ref.shape[2]
    lanes = swap_ref.shape[0]
    across = (((1,), (1,)), ((), ()))
    for start in range(0, depth, lanes):
        y_ref[:, start : start + lanes] = jnp.dot(
            x_ref[0, :, start : start + lanes], swap_ref[...], preferred_element_type=jnp.float32
        ).astype(jnp.bfloat16)

    def rows(step, carry):
        at = pl.ds(pl.multiple_of(step * tile, tile), tile)
        re = lax.dot_general(x_ref[0, at, :], x_ref[0], across, preferred_element_type=jnp.float32)
        vis_ref[0, 0, at, :] = (re / frame_count).astype(vis_ref.dtype)
        im = lax.dot_general(y_ref[at, :], x_ref[0], across, preferred_element_type=jnp.float32)
        vis_ref[1, 0, at, :] = (im / frame_count).astype(vis_ref.dtype)
        return carry

    lax.fori_loop(0, inputs // tile, rows, 0)
    power_ref[...] = jnp.zeros_like(power_ref)
    width = 4 * lanes if depth % (4 * lanes) == 0 else lanes

    def columns(step, carry):
        at = pl.ds(pl.multiple_of(step * width, width), width)
        beam = jnp.dot(w_ref[0, 0], x_ref[0, :, at], preferred_element_type=jnp.float32)
        beam = beam - jnp.dot(w_ref[1, 0], y_ref[:, at], preferred_element_type=jnp.float32)
        square = beam * beam
        high = square.astype(jnp.bfloat16)
        low = (square - high.astype(jnp.float32)).astype(jnp.bfloat16)
        pool = pool_ref[at, :]
        power_ref[0] += jnp.dot(high, pool, preferred_element_type=jnp.float32) + jnp.dot(
            low, pool, preferred_element_type=jnp.float32
        )
        return carry

    lax.fori_loop(0, depth // width, columns, 0)


def products(x, weights, frames):
    own, inputs, depth = x.shape
    beams = weights.shape[2]
    bins = depth // (2 * INTEG)
    lanes = 2 * frames
    source = jnp.arange(lanes)[:, None]
    goal = jnp.arange(lanes)[None, :]
    swap = jnp.where(source == goal + frames, 1.0, 0.0) - jnp.where(source + frames == goal, 1.0, 0.0)
    at = jnp.arange(depth)
    frame = at // lanes * frames + at % frames
    pool = jnp.where(frame[:, None] // INTEG == jnp.arange(bins)[None, :], 1.0 / INTEG, 0.0)
    return pl.pallas_call(
        functools.partial(products_kernel, depth // 2, min(inputs, 256)),
        grid=(own,),
        out_shape=(
            jax.ShapeDtypeStruct((2, own, inputs, inputs), jnp.bfloat16),
            jax.ShapeDtypeStruct((own, beams, bins), jnp.float32),
        ),
        in_specs=[
            pl.BlockSpec((1, inputs, depth), lambda j: (j, 0, 0)),
            pl.BlockSpec((2, 1, beams, inputs), lambda j: (0, j, 0, 0)),
            pl.BlockSpec((lanes, lanes), lambda j: (0, 0)),
            pl.BlockSpec((depth, bins), lambda j: (0, 0)),
        ],
        out_specs=(
            pl.BlockSpec((2, 1, inputs, inputs), lambda j: (0, j, 0, 0)),
            pl.BlockSpec((1, beams, bins), lambda j: (j, 0, 0)),
        ),
        scratch_shapes=[pltpu.VMEM((inputs, depth), jnp.bfloat16)],
        compiler_params=pltpu.CompilerParams(vmem_limit_bytes=60 << 20),
        name="products",
    )(x, weights, swap.astype(jnp.bfloat16), pool.astype(jnp.bfloat16))


def by_channels(voltages, input_flags, channel_order, beam_weights):
    _, rs, qs = sizes()
    spectrum = channelize(voltages, input_flags, channel_order)
    frames = spectrum.shape[2] // 2
    x, weights = turn(spectrum, beam_weights)
    visibility, power = products(x, weights, frames)
    own, beams, bins = power.shape
    split = power.reshape(own, qs, beams // qs, rs, bins // rs)
    parts = jnp.transpose(split, (3, 1, 0, 2, 4)).reshape(rs * qs, -1, 2 * frames)
    block, part = deliver(visibility, parts)
    beam_power = part.reshape(rs * qs * own, beams // qs, bins // rs)
    return (block.astype(jnp.float32), beam_power)


def on_device(voltages, input_flags, channel_order, beam_weights):
    cs, rs, qs = sizes()
    lanes = 2 * (voltages.shape[2] // NCH)
    if NCH % (cs * rs * qs) == 0 and lanes % 128 == 0:
        plan = by_channels
    else:
        plan = by_panels
    return plan(voltages, input_flags, channel_order, beam_weights)


def solution(mesh):
    placed = (P(None, "chan", ("row", "col")), P("chan"), P(), P(None, "chan", "col", None))
    return jax.shard_map(
        on_device,
        mesh=mesh,
        in_specs=placed,
        out_specs=(P(None, "chan", "row", "col"), P("chan", "col", "row")),
        check_vma=False,
    )
```

```python
import functools
import math

import jax
import jax.numpy as jnp
from jax import lax
from jax.experimental import pallas as pl
from jax.experimental.pallas import tpu as pltpu
from jax.sharding import PartitionSpec as P

NCH = 128
TAPS = 4
INTEG = 8


def passed_along(value, axis, steps):
    count = lax.axis_size(axis)
    initial, last = (max(0, -steps), min(count, count - steps))
    return lax.ppermute(value, axis, [(source, source + steps) for source in range(initial, last)])


def prototype(taps, length):
    position = jnp.arange(taps * length, dtype=jnp.float32) + 0.5
    offset = position / length - taps / 2.0
    window = 0.5 - 0.5 * jnp.cos(2.0 * math.pi * position / (taps * length))
    return (jnp.sin(math.pi * offset) / (math.pi * offset) * window).reshape(taps, length)


def dft_tables(channel_rows, length):
    sample_index = jnp.arange(length, dtype=jnp.int32)
    product = channel_rows[:, None] * sample_index[None, :] % length
    angle = 2.0 * math.pi / length * product.astype(jnp.float32)
    factor = 1.0 / math.sqrt(length)
    cosine = jnp.cos(angle) * factor
    sine = jnp.sin(angle) * factor
    real_rows = jnp.stack([cosine, sine], axis=1)
    imag_rows = jnp.stack([-sine, cosine], axis=1)
    return jnp.stack([real_rows, imag_rows], axis=1).astype(jnp.bfloat16)


def to_frames(gathered, frames, outer, inner, swapped):
    chans = gathered.shape[0]
    width = gathered.shape[1]
    split = gathered.reshape(chans, width, outer, inner, 2, frames)
    if swapped:
        order = jnp.transpose(split, (0, 4, 1, 3, 2, 5))
    else:
        order = jnp.transpose(split, (0, 4, 1, 2, 3, 5))
    return order.reshape(chans, 2, width, outer * inner * frames)


def correlate_one(left_block, right_block, frame_count):
    left_re = left_block[0]
    left_im = left_block[1]
    right_re = right_block[0]
    right_im = right_block[1]
    dims = (((1,), (1,)), ((), ()))
    vis_re = lax.dot_general(left_re, right_re, dims, preferred_element_type=jnp.float32)
    vis_re = vis_re + lax.dot_general(left_im, right_im, dims, preferred_element_type=jnp.float32)
    vis_im = lax.dot_general(left_im, right_re, dims, preferred_element_type=jnp.float32)
    vis_im = vis_im - lax.dot_general(left_re, right_im, dims, preferred_element_type=jnp.float32)
    return jnp.stack([vis_re, vis_im]) / frame_count


def correlate(left_view, right_view, frame_count):
    result = lax.map(
        lambda items: correlate_one(items[0], items[1], frame_count), (left_view, right_view)
    )
    return jnp.transpose(result, (1, 0, 2, 3))


def beams_one(weights, block):
    w_real = weights[0]
    w_imag = weights[1]
    x_real = block[0]
    x_imag = block[1]
    beam_re = jnp.dot(w_real, x_real, preferred_element_type=jnp.float32) - jnp.dot(
        w_imag, x_imag, preferred_element_type=jnp.float32
    )
    beam_im = jnp.dot(w_real, x_imag, preferred_element_type=jnp.float32) + jnp.dot(
        w_imag, x_real, preferred_element_type=jnp.float32
    )
    return jnp.stack([beam_re, beam_im], axis=1)


def form_beams(weights, view):
    by_channel = jnp.transpose(weights, (1, 0, 2, 3))
    return lax.map(lambda items: beams_one(items[0], items[1]), (by_channel, view))


def integrate(voltage):
    power = voltage[:, :, 0] * voltage[:, :, 0] + voltage[:, :, 1] * voltage[:, :, 1]
    return power.reshape(power.shape[0], power.shape[1], -1, INTEG).mean(axis=-1)


def channelize(voltages, input_flags, channel_order):
    masked = voltages * input_flags.astype(jnp.bfloat16)[None, :, None]
    local_inputs = masked.shape[1]
    frames = masked.shape[2] // NCH
    history = passed_along(masked[:, :, masked.shape[2] - (TAPS - 1) * NCH :], ("row", "col"), 1)
    joined = jnp.concatenate([history, masked], axis=2)
    blocks = joined.reshape(2, local_inputs, frames + TAPS - 1, NCH)
    coeffs = prototype(TAPS, NCH)
    filtered = jnp.zeros((2, local_inputs, frames, NCH), jnp.float32)
    for tap_index in range(TAPS):
        filtered = filtered + coeffs[tap_index] * blocks[
            :, :, tap_index : tap_index + frames
        ].astype(jnp.float32)
    filtered = filtered.astype(jnp.bfloat16)
    tables = dft_tables(channel_order, NCH)
    spectrum = jnp.einsum(
        "kqpn,pifn->kiqf",
        tables.astype(jnp.float32),
        filtered.astype(jnp.float32),
        precision=lax.Precision.HIGHEST,
    ).astype(jnp.bfloat16)
    spectrum = spectrum.reshape(NCH, local_inputs, 2 * frames)
    return spectrum


def by_panels(voltages, input_flags, channel_order, beam_weights):
    spectrum = channelize(voltages, input_flags, channel_order)
    frames = spectrum.shape[2] // 2
    turned = lax.all_to_all(spectrum, "chan", split_axis=0, concat_axis=1, tiled=True)
    row_count = lax.axis_size("row")
    col_count = lax.axis_size("col")
    total_frames = frames * row_count * col_count
    row_turned = lax.all_to_all(turned, "row", split_axis=1, concat_axis=2, tiled=True)
    row_all = lax.all_gather(row_turned, "col", axis=2, tiled=True)
    col_turned = lax.all_to_all(turned, "col", split_axis=1, concat_axis=2, tiled=True)
    col_all = lax.all_gather(col_turned, "row", axis=2, tiled=True)
    row_view = to_frames(row_all, frames, col_count, row_count, True)
    col_view = to_frames(col_all, frames, row_count, col_count, False)
    visibility = correlate(row_view, col_view, total_frames)
    weights_all = lax.all_gather(beam_weights, "col", axis=2, tiled=True)
    local_view = to_frames(turned, frames, 1, 1, False)
    voltage = form_beams(weights_all, local_view)
    own_power = integrate(voltage)
    beam_power = lax.all_to_all(own_power, "col", split_axis=1, concat_axis=2, tiled=True)
    return (visibility, beam_power)


MESH = pl.DeviceIdType.MESH


def spectra_kernel(v_ref, h_ref, flag_ref, coeff_ref, table_ref, out_ref, filtered_ref, wide_ref):
    tile = v_ref.shape[1]
    frames = v_ref.shape[2] // NCH
    lanes = 2 * frames
    flag = jnp.broadcast_to(flag_ref[...], (tile, NCH))
    rows = [jnp.broadcast_to(coeff_ref[tap : tap + 1, :], (tile, NCH)) for tap in range(TAPS)]
    for part in range(2):

        def frame_at(index):
            ref, at = (h_ref, index) if index < TAPS - 1 else (v_ref, index - TAPS + 1)
            return ref[part, :, at * NCH : (at + 1) * NCH].astype(jnp.float32) * flag

        window = [frame_at(index) for index in range(TAPS - 1)]
        for frame in range(frames):
            window = window[-(TAPS - 1) :] + [frame_at(frame + TAPS - 1)]
            total = rows[0] * window[0]
            for tap in range(1, TAPS):
                total = total + rows[tap] * window[tap]
            filtered_ref[part, frame] = total
    for first in range(0, tile, 2):
        stack = []
        for index in (first, first + 1):
            re = filtered_ref[0, :, index, :].astype(jnp.bfloat16)
            im = filtered_ref[1, :, index, :].astype(jnp.bfloat16)
            stack.append(jnp.concatenate([re, im], axis=1))
            stack.append(jnp.concatenate([im, -re], axis=1))
        both = lax.dot_general(
            table_ref[...],
            jnp.concatenate(stack, axis=0),
            (((1,), (1,)), ((), ())),
            preferred_element_type=jnp.float32,
        )
        wide_ref[:, first, :] = both[:, :lanes]
        wide_ref[:, first + 1, :] = both[:, lanes:]
    out_ref[...] = wide_ref[...].astype(out_ref.dtype)


def spectra_of(voltages, input_flags, channel_order):
    _, inputs, samples = voltages.shape
    past = (TAPS - 1) * NCH
    history = passed_along(voltages[:, :, samples - past :], ("row", "col"), 1)
    frames = samples // NCH
    tile = 16
    tables = dft_tables(channel_order, NCH)[:, 0].reshape(NCH, 2 * NCH)
    return pl.pallas_call(
        spectra_kernel,
        grid=(inputs // tile,),
        out_shape=jax.ShapeDtypeStruct((NCH, inputs, 2 * frames), jnp.bfloat16),
        in_specs=[
            pl.BlockSpec((2, tile, samples), lambda i: (0, i, 0)),
            pl.BlockSpec((2, tile, past), lambda i: (0, i, 0)),
            pl.BlockSpec((tile, 1), lambda i: (i, 0)),
            pl.BlockSpec((TAPS, NCH), lambda i: (0, 0)),
            pl.BlockSpec((NCH, 2 * NCH), lambda i: (0, 0)),
        ],
        out_specs=pl.BlockSpec((NCH, tile, 2 * frames), lambda i: (0, i, 0)),
        scratch_shapes=[
            pltpu.VMEM((2, frames, tile, NCH), jnp.float32),
            pltpu.VMEM((NCH, tile, 2 * frames), jnp.float32),
        ],
        name="spectra",
    )(
        voltages,
        history,
        input_flags.astype(jnp.float32)[:, None],
        prototype(TAPS, NCH),
        tables,
    )


def sizes():
    return lax.axis_size("chan"), lax.axis_size("row"), lax.axis_size("col")


def turn_kernel(cs, rs, qs, spec_ref, weight_ref, x_ref, w_ref, send, recv, wsend, wrecv, local):
    c, r, q = (lax.axis_index(name) for name in ("chan", "row", "col"))
    cells = rs * qs
    devices = cs * cells
    me = r * qs + q
    here = c * cells + me
    own = spec_ref.shape[0] // devices
    inputs = spec_ref.shape[1]
    lanes = spec_ref.shape[2]
    beams = weight_ref.shape[2]

    def ahead(step, sign):
        row = (r + rs + sign * (step % rs)) % rs
        return row * qs + (q + qs + sign * (step // rs)) % qs

    def place(chan, cell):
        return x_ref.at[
            :,
            pl.ds(pl.multiple_of(chan * inputs, inputs), inputs),
            pl.ds(pl.multiple_of(cell * lanes, lanes), lanes),
        ]

    def spectra(step, outgoing):
        if outgoing:
            chan, cell = (c + step % cs) % cs, ahead(step // cs, 1)
            target = place(c, me)
            slot = here
        else:
            chan, cell = (c + cs - step % cs) % cs, ahead(step // cs, -1)
            target = place(chan, cell)
            slot = chan * cells + cell
        return pltpu.make_async_remote_copy(
            src_ref=spec_ref.at[pl.ds((chan * cells + cell) * own, own)],
            dst_ref=target,
            send_sem=send.at[chan * cells + cell],
            recv_sem=recv.at[slot],
            device_id=(chan, cell // qs, cell % qs),
            device_id_type=MESH,
        )

    def weights(step, outgoing):
        if outgoing:
            peer = (q + step) % qs
            slot = q
        else:
            peer = (q + qs - step) % qs
            slot = peer
        return pltpu.make_async_remote_copy(
            src_ref=weight_ref.at[:, pl.ds((r * qs + peer) * own, own)],
            dst_ref=w_ref.at[:, :, pl.ds(pl.multiple_of(slot * beams, beams), beams)],
            send_sem=wsend.at[peer],
            recv_sem=wrecv.at[slot],
            device_id=(c, r, peer),
            device_id_type=MESH,
        )

    def start(step, carry):
        spectra(step, True).start()
        return carry

    def start_weights(step, carry):
        weights(step, True).start()
        return carry

    lax.fori_loop(1, devices, start, 0)
    lax.fori_loop(1, qs, start_weights, 0)
    stay = pltpu.make_async_copy(spec_ref.at[pl.ds(here * own, own)], place(c, me), local.at[0])
    keep = pltpu.make_async_copy(
        weight_ref.at[:, pl.ds(me * own, own)],
        w_ref.at[:, :, pl.ds(pl.multiple_of(q * beams, beams), beams)],
        local.at[1],
    )
    stay.start()
    keep.start()

    def finish(step, carry):
        spectra(step, True).wait_send()
        spectra(step, False).wait_recv()
        return carry

    def finish_weights(step, carry):
        weights(step, True).wait_send()
        weights(step, False).wait_recv()
        return carry

    lax.fori_loop(1, devices, finish, 0)
    lax.fori_loop(1, qs, finish_weights, 0)
    stay.wait()
    keep.wait()


def turn(spectrum, beam_weights):
    cs, rs, qs = sizes()
    devices = cs * rs * qs
    own = spectrum.shape[0] // devices
    anywhere = pl.BlockSpec(memory_space=pl.ANY)
    return pl.pallas_call(
        functools.partial(turn_kernel, cs, rs, qs),
        out_shape=(
            jax.ShapeDtypeStruct(
                (own, spectrum.shape[1] * cs, spectrum.shape[2] * rs * qs), spectrum.dtype
            ),
            jax.ShapeDtypeStruct(
                (2, own, beam_weights.shape[2] * qs, beam_weights.shape[3]), beam_weights.dtype
            ),
        ),
        in_specs=[anywhere] * 2,
        out_specs=(anywhere,) * 2,
        scratch_shapes=[
            pltpu.SemaphoreType.DMA((devices,)),
            pltpu.SemaphoreType.DMA((devices,)),
            pltpu.SemaphoreType.DMA((qs,)),
            pltpu.SemaphoreType.DMA((qs,)),
            pltpu.SemaphoreType.DMA((2,)),
        ],
        compiler_params=pltpu.CompilerParams(has_side_effects=True),
        name="turn",
    )(spectrum, beam_weights)


def deliver_kernel(rs, qs, vis_ref, power_ref, block_ref, part_ref, send, recv, psend, precv, local):
    c, r, q = (lax.axis_index(name) for name in ("chan", "row", "col"))
    cells = rs * qs
    me = r * qs + q
    own, height, width = vis_ref.shape[1], block_ref.shape[2], block_ref.shape[3]

    def ahead(step, sign):
        row = (r + rs + sign * (step % rs)) % rs
        return row * qs + (q + qs + sign * (step // rs)) % qs

    def piece(row, col):
        return vis_ref.at[
            :,
            :,
            pl.ds(pl.multiple_of(row * height, height), height),
            pl.ds(pl.multiple_of(col * width, width), width),
        ]

    def copies(step, outgoing):
        if outgoing:
            cell = ahead(step, 1)
            slot = me
        else:
            cell = ahead(step, -1)
            slot = cell
        device = (c, cell // qs, cell % qs)
        block = pltpu.make_async_remote_copy(
            src_ref=piece(cell // qs, cell % qs),
            dst_ref=block_ref.at[:, pl.ds(slot * own, own)],
            send_sem=send.at[cell],
            recv_sem=recv.at[slot],
            device_id=device,
            device_id_type=MESH,
        )
        part = pltpu.make_async_remote_copy(
            src_ref=power_ref.at[cell],
            dst_ref=part_ref.at[slot],
            send_sem=psend.at[cell],
            recv_sem=precv.at[slot],
            device_id=device,
            device_id_type=MESH,
        )
        return block, part

    def start(step, carry):
        for copy in copies(step, True):
            copy.start()
        return carry

    lax.fori_loop(1, cells, start, 0)
    stay = pltpu.make_async_copy(piece(r, q), block_ref.at[:, pl.ds(me * own, own)], local.at[0])
    keep = pltpu.make_async_copy(power_ref.at[me], part_ref.at[me], local.at[1])
    stay.start()
    keep.start()

    def finish(step, carry):
        for copy in copies(step, True):
            copy.wait_send()
        for copy in copies(step, False):
            copy.wait_recv()
        return carry

    lax.fori_loop(1, cells, finish, 0)
    stay.wait()
    keep.wait()


def deliver(visibility, power):
    _, rs, qs = sizes()
    cells = rs * qs
    own = visibility.shape[1]
    anywhere = pl.BlockSpec(memory_space=pl.ANY)
    return pl.pallas_call(
        functools.partial(deliver_kernel, rs, qs),
        out_shape=(
            jax.ShapeDtypeStruct(
                (2, own * cells, visibility.shape[2] // rs, visibility.shape[3] // qs),
                visibility.dtype,
            ),
            jax.ShapeDtypeStruct(power.shape, power.dtype),
        ),
        in_specs=[anywhere] * 2,
        out_specs=(anywhere,) * 2,
        scratch_shapes=[pltpu.SemaphoreType.DMA((cells,))] * 4 + [pltpu.SemaphoreType.DMA((2,))],
        compiler_params=pltpu.CompilerParams(has_side_effects=True),
        name="deliver",
    )(visibility, power)


def products_kernel(frame_count, tile, x_ref, w_ref, swap_ref, pool_ref, vis_ref, power_ref, y_ref):
    inputs, depth = x_ref.shape[1], x_ref.shape[2]
    lanes = swap_ref.shape[0]
    across = (((1,), (1,)), ((), ()))
    for start in range(0, depth, lanes):
        y_ref[:, start : start + lanes] = jnp.dot(
            x_ref[0, :, start : start + lanes], swap_ref[...], preferred_element_type=jnp.float32
        ).astype(jnp.bfloat16)

    def rows(step, carry):
        at = pl.ds(pl.multiple_of(step * tile, tile), tile)
        re = lax.dot_general(x_ref[0, at, :], x_ref[0], across, preferred_element_type=jnp.float32)
        vis_ref[0, 0, at, :] = (re / frame_count).astype(vis_ref.dtype)
        im = lax.dot_general(y_ref[at, :], x_ref[0], across, preferred_element_type=jnp.float32)
        vis_ref[1, 0, at, :] = (im / frame_count).astype(vis_ref.dtype)
        return carry

    lax.fori_loop(0, inputs // tile, rows, 0)
    power_ref[...] = jnp.zeros_like(power_ref)
    width = 4 * lanes if depth % (4 * lanes) == 0 else lanes

    def columns(step, carry):
        at = pl.ds(pl.multiple_of(step * width, width), width)
        beam = jnp.dot(w_ref[0, 0], x_ref[0, :, at], preferred_element_type=jnp.float32)
        beam = beam - jnp.dot(w_ref[1, 0], y_ref[:, at], preferred_element_type=jnp.float32)
        square = beam * beam
        high = square.astype(jnp.bfloat16)
        low = (square - high.astype(jnp.float32)).astype(jnp.bfloat16)
        pool = pool_ref[at, :]
        power_ref[0] += jnp.dot(high, pool, preferred_element_type=jnp.float32) + jnp.dot(
            low, pool, preferred_element_type=jnp.float32
        )
        return carry

    lax.fori_loop(0, depth // width, columns, 0)


def products(x, weights, frames):
    own, inputs, depth = x.shape
    beams = weights.shape[2]
    bins = depth // (2 * INTEG)
    lanes = 2 * frames
    source = jnp.arange(lanes)[:, None]
    goal = jnp.arange(lanes)[None, :]
    swap = jnp.where(source == goal + frames, 1.0, 0.0) - jnp.where(source + frames == goal, 1.0, 0.0)
    at = jnp.arange(depth)
    frame = at // lanes * frames + at % frames
    pool = jnp.where(frame[:, None] // INTEG == jnp.arange(bins)[None, :], 1.0 / INTEG, 0.0)
    return pl.pallas_call(
        functools.partial(products_kernel, depth // 2, min(inputs, 256)),
        grid=(own,),
        out_shape=(
            jax.ShapeDtypeStruct((2, own, inputs, inputs), jnp.bfloat16),
            jax.ShapeDtypeStruct((own, beams, bins), jnp.float32),
        ),
        in_specs=[
            pl.BlockSpec((1, inputs, depth), lambda j: (j, 0, 0)),
            pl.BlockSpec((2, 1, beams, inputs), lambda j: (0, j, 0, 0)),
            pl.BlockSpec((lanes, lanes), lambda j: (0, 0)),
            pl.BlockSpec((depth, bins), lambda j: (0, 0)),
        ],
        out_specs=(
            pl.BlockSpec((2, 1, inputs, inputs), lambda j: (0, j, 0, 0)),
            pl.BlockSpec((1, beams, bins), lambda j: (j, 0, 0)),
        ),
        scratch_shapes=[pltpu.VMEM((inputs, depth), jnp.bfloat16)],
        compiler_params=pltpu.CompilerParams(vmem_limit_bytes=60 << 20),
        name="products",
    )(x, weights, swap.astype(jnp.bfloat16), pool.astype(jnp.bfloat16))


def by_channels(voltages, input_flags, channel_order, beam_weights):
    _, rs, qs = sizes()
    spectrum = spectra_of(voltages, input_flags, channel_order)
    frames = spectrum.shape[2] // 2
    x, weights = turn(spectrum, beam_weights)
    visibility, power = products(x, weights, frames)
    own, beams, bins = power.shape
    split = power.reshape(own, qs, beams // qs, rs, bins // rs)
    parts = jnp.transpose(split, (3, 1, 0, 2, 4)).reshape(rs * qs, -1, 2 * frames)
    block, part = deliver(visibility, parts)
    beam_power = part.reshape(rs * qs * own, beams // qs, bins // rs)
    return (block.astype(jnp.float32), beam_power)


def on_device(voltages, input_flags, channel_order, beam_weights):
    cs, rs, qs = sizes()
    lanes = 2 * (voltages.shape[2] // NCH)
    if NCH % (cs * rs * qs) == 0 and lanes % 128 == 0 and voltages.shape[1] % 16 == 0:
        plan = by_channels
    else:
        plan = by_panels
    return plan(voltages, input_flags, channel_order, beam_weights)


def solution(mesh):
    placed = (P(None, "chan", ("row", "col")), P("chan"), P(), P(None, "chan", "col", None))
    return jax.shard_map(
        on_device,
        mesh=mesh,
        in_specs=placed,
        out_specs=(P(None, "chan", "row", "col"), P("chan", "col", "row")),
        check_vma=False,
    )
```

```python
import functools
import math

import jax
import jax.numpy as jnp
from jax import lax
from jax.experimental import pallas as pl
from jax.experimental.pallas import tpu as pltpu
from jax.sharding import PartitionSpec as P

NCH = 128
TAPS = 4
INTEG = 8


def passed_along(value, axis, steps):
    count = lax.axis_size(axis)
    initial, last = (max(0, -steps), min(count, count - steps))
    return lax.ppermute(value, axis, [(source, source + steps) for source in range(initial, last)])


def prototype(taps, length):
    position = jnp.arange(taps * length, dtype=jnp.float32) + 0.5
    offset = position / length - taps / 2.0
    window = 0.5 - 0.5 * jnp.cos(2.0 * math.pi * position / (taps * length))
    return (jnp.sin(math.pi * offset) / (math.pi * offset) * window).reshape(taps, length)


def dft_tables(channel_rows, length):
    sample_index = jnp.arange(length, dtype=jnp.int32)
    product = channel_rows[:, None] * sample_index[None, :] % length
    angle = 2.0 * math.pi / length * product.astype(jnp.float32)
    factor = 1.0 / math.sqrt(length)
    cosine = jnp.cos(angle) * factor
    sine = jnp.sin(angle) * factor
    real_rows = jnp.stack([cosine, sine], axis=1)
    imag_rows = jnp.stack([-sine, cosine], axis=1)
    return jnp.stack([real_rows, imag_rows], axis=1).astype(jnp.bfloat16)


def to_frames(gathered, frames, outer, inner, swapped):
    chans = gathered.shape[0]
    width = gathered.shape[1]
    split = gathered.reshape(chans, width, outer, inner, 2, frames)
    if swapped:
        order = jnp.transpose(split, (0, 4, 1, 3, 2, 5))
    else:
        order = jnp.transpose(split, (0, 4, 1, 2, 3, 5))
    return order.reshape(chans, 2, width, outer * inner * frames)


def correlate_one(left_block, right_block, frame_count):
    left_re = left_block[0]
    left_im = left_block[1]
    right_re = right_block[0]
    right_im = right_block[1]
    dims = (((1,), (1,)), ((), ()))
    vis_re = lax.dot_general(left_re, right_re, dims, preferred_element_type=jnp.float32)
    vis_re = vis_re + lax.dot_general(left_im, right_im, dims, preferred_element_type=jnp.float32)
    vis_im = lax.dot_general(left_im, right_re, dims, preferred_element_type=jnp.float32)
    vis_im = vis_im - lax.dot_general(left_re, right_im, dims, preferred_element_type=jnp.float32)
    return jnp.stack([vis_re, vis_im]) / frame_count


def correlate(left_view, right_view, frame_count):
    result = lax.map(
        lambda items: correlate_one(items[0], items[1], frame_count), (left_view, right_view)
    )
    return jnp.transpose(result, (1, 0, 2, 3))


def beams_one(weights, block):
    w_real = weights[0]
    w_imag = weights[1]
    x_real = block[0]
    x_imag = block[1]
    beam_re = jnp.dot(w_real, x_real, preferred_element_type=jnp.float32) - jnp.dot(
        w_imag, x_imag, preferred_element_type=jnp.float32
    )
    beam_im = jnp.dot(w_real, x_imag, preferred_element_type=jnp.float32) + jnp.dot(
        w_imag, x_real, preferred_element_type=jnp.float32
    )
    return jnp.stack([beam_re, beam_im], axis=1)


def form_beams(weights, view):
    by_channel = jnp.transpose(weights, (1, 0, 2, 3))
    return lax.map(lambda items: beams_one(items[0], items[1]), (by_channel, view))


def integrate(voltage):
    power = voltage[:, :, 0] * voltage[:, :, 0] + voltage[:, :, 1] * voltage[:, :, 1]
    return power.reshape(power.shape[0], power.shape[1], -1, INTEG).mean(axis=-1)


def channelize(voltages, input_flags, channel_order):
    masked = voltages * input_flags.astype(jnp.bfloat16)[None, :, None]
    local_inputs = masked.shape[1]
    frames = masked.shape[2] // NCH
    history = passed_along(masked[:, :, masked.shape[2] - (TAPS - 1) * NCH :], ("row", "col"), 1)
    joined = jnp.concatenate([history, masked], axis=2)
    blocks = joined.reshape(2, local_inputs, frames + TAPS - 1, NCH)
    coeffs = prototype(TAPS, NCH)
    filtered = jnp.zeros((2, local_inputs, frames, NCH), jnp.float32)
    for tap_index in range(TAPS):
        filtered = filtered + coeffs[tap_index] * blocks[
            :, :, tap_index : tap_index + frames
        ].astype(jnp.float32)
    filtered = filtered.astype(jnp.bfloat16)
    tables = dft_tables(channel_order, NCH)
    spectrum = jnp.einsum(
        "kqpn,pifn->kiqf",
        tables.astype(jnp.float32),
        filtered.astype(jnp.float32),
        precision=lax.Precision.HIGHEST,
    ).astype(jnp.bfloat16)
    spectrum = spectrum.reshape(NCH, local_inputs, 2 * frames)
    return spectrum


def by_panels(voltages, input_flags, channel_order, beam_weights):
    spectrum = channelize(voltages, input_flags, channel_order)
    frames = spectrum.shape[2] // 2
    turned = lax.all_to_all(spectrum, "chan", split_axis=0, concat_axis=1, tiled=True)
    row_count = lax.axis_size("row")
    col_count = lax.axis_size("col")
    total_frames = frames * row_count * col_count
    row_turned = lax.all_to_all(turned, "row", split_axis=1, concat_axis=2, tiled=True)
    row_all = lax.all_gather(row_turned, "col", axis=2, tiled=True)
    col_turned = lax.all_to_all(turned, "col", split_axis=1, concat_axis=2, tiled=True)
    col_all = lax.all_gather(col_turned, "row", axis=2, tiled=True)
    row_view = to_frames(row_all, frames, col_count, row_count, True)
    col_view = to_frames(col_all, frames, row_count, col_count, False)
    visibility = correlate(row_view, col_view, total_frames)
    weights_all = lax.all_gather(beam_weights, "col", axis=2, tiled=True)
    local_view = to_frames(turned, frames, 1, 1, False)
    voltage = form_beams(weights_all, local_view)
    own_power = integrate(voltage)
    beam_power = lax.all_to_all(own_power, "col", split_axis=1, concat_axis=2, tiled=True)
    return (visibility, beam_power)


MESH = pl.DeviceIdType.MESH


def spectra_tile(v_ref, h_ref, flag_ref, coeff_ref, table_ref, filtered_ref, wide_ref):
    tile = v_ref.shape[1]
    frames = v_ref.shape[2] // NCH
    lanes = 2 * frames
    flag = jnp.broadcast_to(flag_ref[...], (tile, NCH))
    rows = [jnp.broadcast_to(coeff_ref[tap : tap + 1, :], (tile, NCH)) for tap in range(TAPS)]
    for part in range(2):

        def frame_at(index):
            ref, at = (h_ref, index) if index < TAPS - 1 else (v_ref, index - TAPS + 1)
            return ref[part, :, at * NCH : (at + 1) * NCH].astype(jnp.float32) * flag

        window = [frame_at(index) for index in range(TAPS - 1)]
        for frame in range(frames):
            window = window[-(TAPS - 1) :] + [frame_at(frame + TAPS - 1)]
            total = rows[0] * window[0]
            for tap in range(1, TAPS):
                total = total + rows[tap] * window[tap]
            filtered_ref[part, frame] = total
    for first in range(0, tile, 2):
        stack = []
        for index in (first, first + 1):
            re = filtered_ref[0, :, index, :].astype(jnp.bfloat16)
            im = filtered_ref[1, :, index, :].astype(jnp.bfloat16)
            stack.append(jnp.concatenate([re, im], axis=1))
            stack.append(jnp.concatenate([im, -re], axis=1))
        both = lax.dot_general(
            table_ref[...],
            jnp.concatenate(stack, axis=0),
            (((1,), (1,)), ((), ())),
            preferred_element_type=jnp.float32,
        )
        wide_ref[:, first, :] = both[:, :lanes]
        wide_ref[:, first + 1, :] = both[:, lanes:]
    return wide_ref[...].astype(jnp.bfloat16)


def sizes():
    return lax.axis_size("chan"), lax.axis_size("row"), lax.axis_size("col")


def turn_kernel(
    cs, rs, qs, tile, group,
    v_ref, h_ref, flag_ref, coeff_ref, table_ref, weight_ref, x_ref, w_ref,
    filtered_ref, wide_ref, spec_ref, send, recv, wsend, wrecv, local,
):
    c, r, q = (lax.axis_index(name) for name in ("chan", "row", "col"))
    cells = rs * qs
    devices = cs * cells
    me = r * qs + q
    here = c * cells + me
    own = spec_ref.shape[0] // devices
    inputs = spec_ref.shape[1]
    lanes = spec_ref.shape[2]
    beams = weight_ref.shape[2]
    turn_step = pl.program_id(0)
    tiles = inputs // tile

    def ahead(step, sign):
        row = (r + rs + sign * (step % rs)) % rs
        return row * qs + (q + qs + sign * (step // rs)) % qs

    def spectra(step, outgoing, first, count):
        if outgoing:
            chan, cell = (c + step % cs) % cs, ahead(step // cs, 1)
            origin, column = c, me
            slot = here
        else:
            chan, cell = (c + cs - step % cs) % cs, ahead(step // cs, -1)
            origin, column = chan, cell
            slot = chan * cells + cell
        return pltpu.make_async_remote_copy(
            src_ref=spec_ref.at[
                pl.ds((chan * cells + cell) * own, own),
                pl.ds(pl.multiple_of(first, tile), count),
            ],
            dst_ref=x_ref.at[
                :,
                pl.ds(pl.multiple_of(origin * inputs + first, tile), count),
                pl.ds(pl.multiple_of(column * lanes, lanes), lanes),
            ],
            send_sem=send.at[chan * cells + cell],
            recv_sem=recv.at[slot],
            device_id=(chan, cell // qs, cell % qs),
            device_id_type=MESH,
        )

    def weights(step, outgoing):
        if outgoing:
            peer = (q + step) % qs
            slot = q
        else:
            peer = (q + qs - step) % qs
            slot = peer
        return pltpu.make_async_remote_copy(
            src_ref=weight_ref.at[:, pl.ds((r * qs + peer) * own, own)],
            dst_ref=w_ref.at[:, :, pl.ds(pl.multiple_of(slot * beams, beams), beams)],
            send_sem=wsend.at[peer],
            recv_sem=wrecv.at[slot],
            device_id=(c, r, peer),
            device_id_type=MESH,
        )

    keep = pltpu.make_async_copy(
        weight_ref.at[:, pl.ds(me * own, own)],
        w_ref.at[:, :, pl.ds(pl.multiple_of(q * beams, beams), beams)],
        local.at[1],
    )

    @pl.when(turn_step == 0)
    def _():
        def start_weights(step, carry):
            weights(step, True).start()
            return carry

        lax.fori_loop(1, qs, start_weights, 0)
        keep.start()

    @pl.when((turn_step > 0) & (turn_step * tile % group == 0))
    def _():
        def start(step, carry):
            spectra(step, True, turn_step * tile - group, group).start()
            return carry

        lax.fori_loop(1, devices, start, 0)

    @pl.when(turn_step < tiles)
    def _():
        at = pl.ds(pl.multiple_of(turn_step * tile, tile), tile)
        spec_ref[:, at, :] = spectra_tile(
            v_ref, h_ref, flag_ref, coeff_ref, table_ref, filtered_ref, wide_ref
        )

    @pl.when(turn_step == tiles)
    def _():
        stay = pltpu.make_async_copy(
            spec_ref.at[pl.ds(here * own, own)],
            x_ref.at[
                :,
                pl.ds(pl.multiple_of(c * inputs, inputs), inputs),
                pl.ds(pl.multiple_of(me * lanes, lanes), lanes),
            ],
            local.at[0],
        )
        stay.start()

        def finish(step, carry):
            spectra(step, True, 0, inputs).wait_send()
            spectra(step, False, 0, inputs).wait_recv()
            return carry

        def finish_weights(step, carry):
            weights(step, True).wait_send()
            weights(step, False).wait_recv()
            return carry

        lax.fori_loop(1, devices, finish, 0)
        lax.fori_loop(1, qs, finish_weights, 0)
        stay.wait()
        keep.wait()


def turn(voltages, input_flags, channel_order, beam_weights):
    cs, rs, qs = sizes()
    devices = cs * rs * qs
    own = NCH // devices
    _, inputs, samples = voltages.shape
    past = (TAPS - 1) * NCH
    history = passed_along(voltages[:, :, samples - past :], ("row", "col"), 1)
    frames = samples // NCH
    lanes = 2 * frames
    tile = 16
    group = 4 * tile if inputs % (4 * tile) == 0 else tile
    last = inputs // tile - 1
    tables = dft_tables(channel_order, NCH)[:, 0].reshape(NCH, 2 * NCH)
    anywhere = pl.BlockSpec(memory_space=pl.ANY)
    return pl.pallas_call(
        functools.partial(turn_kernel, cs, rs, qs, tile, group),
        grid=(inputs // tile + 1,),
        out_shape=(
            jax.ShapeDtypeStruct((own, inputs * cs, lanes * rs * qs), jnp.bfloat16),
            jax.ShapeDtypeStruct(
                (2, own, beam_weights.shape[2] * qs, beam_weights.shape[3]), beam_weights.dtype
            ),
        ),
        in_specs=[
            pl.BlockSpec((2, tile, samples), lambda i: (0, jnp.minimum(i, last), 0)),
            pl.BlockSpec((2, tile, past), lambda i: (0, jnp.minimum(i, last), 0)),
            pl.BlockSpec((tile, 1), lambda i: (jnp.minimum(i, last), 0)),
            pl.BlockSpec((TAPS, NCH), lambda i: (0, 0)),
            pl.BlockSpec((NCH, 2 * NCH), lambda i: (0, 0)),
            anywhere,
        ],
        out_specs=(anywhere,) * 2,
        scratch_shapes=[
            pltpu.VMEM((2, frames, tile, NCH), jnp.float32),
            pltpu.VMEM((NCH, tile, lanes), jnp.float32),
            pltpu.VMEM((NCH, inputs, lanes), jnp.bfloat16),
            pltpu.SemaphoreType.DMA((devices,)),
            pltpu.SemaphoreType.DMA((devices,)),
            pltpu.SemaphoreType.DMA((qs,)),
            pltpu.SemaphoreType.DMA((qs,)),
            pltpu.SemaphoreType.DMA((2,)),
        ],
        compiler_params=pltpu.CompilerParams(has_side_effects=True, vmem_limit_bytes=60 << 20),
        name="turn",
    )(
        voltages,
        history,
        input_flags.astype(jnp.float32)[:, None],
        prototype(TAPS, NCH),
        tables,
        beam_weights,
    )


def products_kernel(
    rs, qs, frame_count, tile,
    x_ref, w_ref, swap_ref, pool_ref, block_ref, part_ref,
    y_ref, vis_ref, power_ref, send, recv, psend, precv, local,
):
    c, r, q = (lax.axis_index(name) for name in ("chan", "row", "col"))
    cells = rs * qs
    me = r * qs + q
    own, inputs = vis_ref.shape[0], vis_ref.shape[2]
    depth = x_ref.shape[2]
    height, width = block_ref.shape[2], block_ref.shape[3]
    part_height, part_width = part_ref.shape[1], part_ref.shape[2]
    channel = pl.program_id(0)

    def ahead(step, sign):
        row = (r + rs + sign * (step % rs)) % rs
        return row * qs + (q + qs + sign * (step // rs)) % qs

    def vis_at(first, count, row, col):
        return vis_ref.at[
            pl.ds(first, count),
            :,
            pl.ds(pl.multiple_of(row * height, height), height),
            pl.ds(pl.multiple_of(col * width, width), width),
        ]

    def power_at(row, col):
        return power_ref.at[
            pl.ds(pl.multiple_of(col * part_height, part_height), part_height),
            pl.ds(pl.multiple_of(row * part_width, part_width), part_width),
        ]

    def ends(step, outgoing):
        if outgoing:
            cell = ahead(step, 1)
            return cell, me
        cell = ahead(step, -1)
        return cell, cell

    def block(step, outgoing, first, count):
        cell, slot = ends(step, outgoing)
        return pltpu.make_async_remote_copy(
            src_ref=vis_at(first, count, cell // qs, cell % qs),
            dst_ref=block_ref.at[pl.ds(slot * own + first, count)],
            send_sem=send.at[cell],
            recv_sem=recv.at[slot],
            device_id=(c, cell // qs, cell % qs),
            device_id_type=MESH,
        )

    def part(step, outgoing):
        cell, slot = ends(step, outgoing)
        return pltpu.make_async_remote_copy(
            src_ref=power_at(cell // qs, cell % qs),
            dst_ref=part_ref.at[slot],
            send_sem=psend.at[cell],
            recv_sem=precv.at[slot],
            device_id=(c, cell // qs, cell % qs),
            device_id_type=MESH,
        )

    @pl.when(channel == 0)
    def _():
        power_ref[...] = jnp.zeros_like(power_ref)

    @pl.when(channel > 0)
    def _():
        def start(step, carry):
            block(step, True, channel - 1, 1).start()
            return carry

        lax.fori_loop(1, cells, start, 0)

    @pl.when(channel < own)
    def _():
        lanes = swap_ref.shape[0]
        across = (((1,), (1,)), ((), ()))

        def rows(step, carry):
            at = pl.ds(pl.multiple_of(step * tile, tile), tile)
            for start in range(0, depth, lanes):
                y_ref[at, start : start + lanes] = jnp.dot(
                    x_ref[0, at, start : start + lanes],
                    swap_ref[...],
                    preferred_element_type=jnp.float32,
                ).astype(jnp.bfloat16)
            re = lax.dot_general(
                x_ref[0, at, :], x_ref[0], across, preferred_element_type=jnp.float32
            )
            vis_ref[channel, 0, at, :] = (re / frame_count).astype(vis_ref.dtype)
            im = lax.dot_general(y_ref[at, :], x_ref[0], across, preferred_element_type=jnp.float32)
            vis_ref[channel, 1, at, :] = (im / frame_count).astype(vis_ref.dtype)
            return carry

        lax.fori_loop(0, inputs // tile, rows, 0)
        span = 4 * lanes if depth % (4 * lanes) == 0 else lanes

        def columns(step, carry):
            at = pl.ds(pl.multiple_of(step * span, span), span)
            beam = jnp.dot(w_ref[0, 0], x_ref[0, :, at], preferred_element_type=jnp.float32)
            beam = beam - jnp.dot(w_ref[1, 0], y_ref[:, at], preferred_element_type=jnp.float32)
            square = beam * beam
            high = square.astype(jnp.bfloat16)
            low = (square - high.astype(jnp.float32)).astype(jnp.bfloat16)
            pool = pool_ref[at, :]
            return (
                carry
                + jnp.dot(high, pool, preferred_element_type=jnp.float32)
                + jnp.dot(low, pool, preferred_element_type=jnp.float32)
            )

        found = lax.fori_loop(0, depth // span, columns, jnp.zeros(power_ref.shape, jnp.float32))
        lane = lax.broadcasted_iota(jnp.int32, power_ref.shape, 1) % part_width
        power_ref[...] = jnp.where(lane // (part_width // own) == channel, found, power_ref[...])

    @pl.when(channel == own)
    def _():
        stay = pltpu.make_async_copy(
            vis_at(0, own, r, q), block_ref.at[pl.ds(me * own, own)], local.at[0]
        )
        keep = pltpu.make_async_copy(power_at(r, q), part_ref.at[me], local.at[1])

        def start(step, carry):
            part(step, True).start()
            return carry

        lax.fori_loop(1, cells, start, 0)
        stay.start()
        keep.start()

        def finish(step, carry):
            block(step, True, 0, own).wait_send()
            block(step, False, 0, own).wait_recv()
            part(step, True).wait_send()
            part(step, False).wait_recv()
            return carry

        lax.fori_loop(1, cells, finish, 0)
        stay.wait()
        keep.wait()


def products(x, weights, frames):
    _, rs, qs = sizes()
    cells = rs * qs
    own, inputs, depth = x.shape
    beams = weights.shape[2]
    bins = depth // (2 * INTEG)
    lanes = 2 * frames
    last = own - 1
    source = jnp.arange(lanes)[:, None]
    goal = jnp.arange(lanes)[None, :]
    swap = jnp.where(source == goal + frames, 1.0, 0.0) - jnp.where(source + frames == goal, 1.0, 0.0)
    at = jnp.arange(depth)
    frame = at // lanes * frames + at % frames
    part = bins // rs
    column = jnp.arange(rs * own * part)
    bin_of = column // (own * part) * part + column % part
    pool = jnp.where(frame[:, None] // INTEG == bin_of[None, :], 1.0 / INTEG, 0.0)
    anywhere = pl.BlockSpec(memory_space=pl.ANY)
    return pl.pallas_call(
        functools.partial(products_kernel, rs, qs, depth // 2, min(inputs, 256)),
        grid=(own + 1,),
        out_shape=(
            jax.ShapeDtypeStruct((cells * own, 2, inputs // rs, inputs // qs), jnp.bfloat16),
            jax.ShapeDtypeStruct((cells, beams // qs, own * part), jnp.float32),
        ),
        in_specs=[
            pl.BlockSpec((1, inputs, depth), lambda j: (jnp.minimum(j, last), 0, 0)),
            pl.BlockSpec((2, 1, beams, inputs), lambda j: (0, jnp.minimum(j, last), 0, 0)),
            pl.BlockSpec((lanes, lanes), lambda j: (0, 0)),
            pl.BlockSpec((depth, rs * own * part), lambda j: (0, 0)),
        ],
        out_specs=(anywhere,) * 2,
        scratch_shapes=[
            pltpu.VMEM((inputs, depth), jnp.bfloat16),
            pltpu.VMEM((own, 2, inputs, inputs), jnp.bfloat16),
            pltpu.VMEM((beams, rs * own * part), jnp.float32),
        ]
        + [pltpu.SemaphoreType.DMA((cells,))] * 4
        + [pltpu.SemaphoreType.DMA((2,))],
        compiler_params=pltpu.CompilerParams(has_side_effects=True, vmem_limit_bytes=60 << 20),
        name="products",
    )(x, weights, swap.astype(jnp.bfloat16), pool.astype(jnp.bfloat16))


def by_channels(voltages, input_flags, channel_order, beam_weights):
    x, weights = turn(voltages, input_flags, channel_order, beam_weights)
    block, part = products(x, weights, voltages.shape[2] // NCH)
    own = x.shape[0]
    cells, beams, _ = part.shape
    split = part.reshape(cells, beams, own, -1)
    beam_power = jnp.transpose(split, (0, 2, 1, 3)).reshape(cells * own, beams, -1)
    visibility = jnp.transpose(block.astype(jnp.float32), (1, 0, 2, 3))
    return (visibility, beam_power)


def on_device(voltages, input_flags, channel_order, beam_weights):
    cs, rs, qs = sizes()
    lanes = 2 * (voltages.shape[2] // NCH)
    devices = cs * rs * qs
    whole = NCH % devices == 0 and lanes % 128 == 0 and voltages.shape[1] % 16 == 0
    if whole and NCH // devices * (lanes // 2 * qs // INTEG) % 128 == 0:
        plan = by_channels
    else:
        plan = by_panels
    return plan(voltages, input_flags, channel_order, beam_weights)


def solution(mesh):
    placed = (P(None, "chan", ("row", "col")), P("chan"), P(), P(None, "chan", "col", None))
    return jax.shard_map(
        on_device,
        mesh=mesh,
        in_specs=placed,
        out_specs=(P(None, "chan", "row", "col"), P("chan", "col", "row")),
        check_vma=False,
    )
```

```python
import functools
import math

import jax
import jax.numpy as jnp
from jax import lax
from jax.experimental import pallas as pl
from jax.experimental.pallas import tpu as pltpu
from jax.sharding import PartitionSpec as P

NCH = 128
TAPS = 4
INTEG = 8


def passed_along(value, axis, steps):
    count = lax.axis_size(axis)
    initial, last = (max(0, -steps), min(count, count - steps))
    return lax.ppermute(value, axis, [(source, source + steps) for source in range(initial, last)])


def prototype(taps, length):
    position = jnp.arange(taps * length, dtype=jnp.float32) + 0.5
    offset = position / length - taps / 2.0
    window = 0.5 - 0.5 * jnp.cos(2.0 * math.pi * position / (taps * length))
    return (jnp.sin(math.pi * offset) / (math.pi * offset) * window).reshape(taps, length)


def dft_tables(channel_rows, length):
    sample_index = jnp.arange(length, dtype=jnp.int32)
    product = channel_rows[:, None] * sample_index[None, :] % length
    angle = 2.0 * math.pi / length * product.astype(jnp.float32)
    factor = 1.0 / math.sqrt(length)
    cosine = jnp.cos(angle) * factor
    sine = jnp.sin(angle) * factor
    real_rows = jnp.stack([cosine, sine], axis=1)
    imag_rows = jnp.stack([-sine, cosine], axis=1)
    return jnp.stack([real_rows, imag_rows], axis=1).astype(jnp.bfloat16)


def to_frames(gathered, frames, outer, inner, swapped):
    chans = gathered.shape[0]
    width = gathered.shape[1]
    split = gathered.reshape(chans, width, outer, inner, 2, frames)
    if swapped:
        order = jnp.transpose(split, (0, 4, 1, 3, 2, 5))
    else:
        order = jnp.transpose(split, (0, 4, 1, 2, 3, 5))
    return order.reshape(chans, 2, width, outer * inner * frames)


def correlate_one(left_block, right_block, frame_count):
    left_re = left_block[0]
    left_im = left_block[1]
    right_re = right_block[0]
    right_im = right_block[1]
    dims = (((1,), (1,)), ((), ()))
    vis_re = lax.dot_general(left_re, right_re, dims, preferred_element_type=jnp.float32)
    vis_re = vis_re + lax.dot_general(left_im, right_im, dims, preferred_element_type=jnp.float32)
    vis_im = lax.dot_general(left_im, right_re, dims, preferred_element_type=jnp.float32)
    vis_im = vis_im - lax.dot_general(left_re, right_im, dims, preferred_element_type=jnp.float32)
    return jnp.stack([vis_re, vis_im]) / frame_count


def correlate(left_view, right_view, frame_count):
    result = lax.map(
        lambda items: correlate_one(items[0], items[1], frame_count), (left_view, right_view)
    )
    return jnp.transpose(result, (1, 0, 2, 3))


def beams_one(weights, block):
    w_real = weights[0]
    w_imag = weights[1]
    x_real = block[0]
    x_imag = block[1]
    beam_re = jnp.dot(w_real, x_real, preferred_element_type=jnp.float32) - jnp.dot(
        w_imag, x_imag, preferred_element_type=jnp.float32
    )
    beam_im = jnp.dot(w_real, x_imag, preferred_element_type=jnp.float32) + jnp.dot(
        w_imag, x_real, preferred_element_type=jnp.float32
    )
    return jnp.stack([beam_re, beam_im], axis=1)


def form_beams(weights, view):
    by_channel = jnp.transpose(weights, (1, 0, 2, 3))
    return lax.map(lambda items: beams_one(items[0], items[1]), (by_channel, view))


def integrate(voltage):
    power = voltage[:, :, 0] * voltage[:, :, 0] + voltage[:, :, 1] * voltage[:, :, 1]
    return power.reshape(power.shape[0], power.shape[1], -1, INTEG).mean(axis=-1)


def channelize(voltages, input_flags, channel_order):
    masked = voltages * input_flags.astype(jnp.bfloat16)[None, :, None]
    local_inputs = masked.shape[1]
    frames = masked.shape[2] // NCH
    history = passed_along(masked[:, :, masked.shape[2] - (TAPS - 1) * NCH :], ("row", "col"), 1)
    joined = jnp.concatenate([history, masked], axis=2)
    blocks = joined.reshape(2, local_inputs, frames + TAPS - 1, NCH)
    coeffs = prototype(TAPS, NCH)
    filtered = jnp.zeros((2, local_inputs, frames, NCH), jnp.float32)
    for tap_index in range(TAPS):
        filtered = filtered + coeffs[tap_index] * blocks[
            :, :, tap_index : tap_index + frames
        ].astype(jnp.float32)
    filtered = filtered.astype(jnp.bfloat16)
    tables = dft_tables(channel_order, NCH)
    spectrum = jnp.einsum(
        "kqpn,pifn->kiqf",
        tables.astype(jnp.float32),
        filtered.astype(jnp.float32),
        precision=lax.Precision.HIGHEST,
    ).astype(jnp.bfloat16)
    spectrum = spectrum.reshape(NCH, local_inputs, 2 * frames)
    return spectrum


def by_panels(voltages, input_flags, channel_order, beam_weights):
    spectrum = channelize(voltages, input_flags, channel_order)
    frames = spectrum.shape[2] // 2
    turned = lax.all_to_all(spectrum, "chan", split_axis=0, concat_axis=1, tiled=True)
    row_count = lax.axis_size("row")
    col_count = lax.axis_size("col")
    total_frames = frames * row_count * col_count
    row_turned = lax.all_to_all(turned, "row", split_axis=1, concat_axis=2, tiled=True)
    row_all = lax.all_gather(row_turned, "col", axis=2, tiled=True)
    col_turned = lax.all_to_all(turned, "col", split_axis=1, concat_axis=2, tiled=True)
    col_all = lax.all_gather(col_turned, "row", axis=2, tiled=True)
    row_view = to_frames(row_all, frames, col_count, row_count, True)
    col_view = to_frames(col_all, frames, row_count, col_count, False)
    visibility = correlate(row_view, col_view, total_frames)
    weights_all = lax.all_gather(beam_weights, "col", axis=2, tiled=True)
    local_view = to_frames(turned, frames, 1, 1, False)
    voltage = form_beams(weights_all, local_view)
    own_power = integrate(voltage)
    beam_power = lax.all_to_all(own_power, "col", split_axis=1, concat_axis=2, tiled=True)
    return (visibility, beam_power)


MESH = pl.DeviceIdType.MESH


def spectra_tile(v_ref, h_ref, flag_ref, coeff_ref, table_ref, filtered_ref, wide_ref):
    tile = v_ref.shape[1]
    frames = v_ref.shape[2] // NCH
    lanes = 2 * frames
    flag = jnp.broadcast_to(flag_ref[...], (tile, NCH))
    rows = [jnp.broadcast_to(coeff_ref[tap : tap + 1, :], (tile, NCH)) for tap in range(TAPS)]
    for part in range(2):

        def frame_at(index):
            ref, at = (h_ref, index) if index < TAPS - 1 else (v_ref, index - TAPS + 1)
            return ref[part, :, at * NCH : (at + 1) * NCH].astype(jnp.float32) * flag

        window = [frame_at(index) for index in range(TAPS - 1)]
        for frame in range(frames):
            window = window[-(TAPS - 1) :] + [frame_at(frame + TAPS - 1)]
            total = rows[0] * window[0]
            for tap in range(1, TAPS):
                total = total + rows[tap] * window[tap]
            filtered_ref[part, frame] = total
    for first in range(0, tile, 2):
        stack = []
        for index in (first, first + 1):
            re = filtered_ref[0, :, index, :].astype(jnp.bfloat16)
            im = filtered_ref[1, :, index, :].astype(jnp.bfloat16)
            stack.append(jnp.concatenate([re, im], axis=1))
            stack.append(jnp.concatenate([im, -re], axis=1))
        both = lax.dot_general(
            table_ref[...],
            jnp.concatenate(stack, axis=0),
            (((1,), (1,)), ((), ())),
            preferred_element_type=jnp.float32,
        )
        wide_ref[:, first, :] = both[:, :lanes]
        wide_ref[:, first + 1, :] = both[:, lanes:]
    return wide_ref[...].astype(jnp.bfloat16)


def sizes():
    return lax.axis_size("chan"), lax.axis_size("row"), lax.axis_size("col")


def turn_kernel(
    cs, rs, qs, tile, group,
    v_ref, h_ref, flag_ref, coeff_ref, table_ref, weight_ref, x_ref, w_ref,
    filtered_ref, wide_ref, spec_ref, send, recv, wsend, wrecv, local,
):
    c, r, q = (lax.axis_index(name) for name in ("chan", "row", "col"))
    cells = rs * qs
    devices = cs * cells
    me = r * qs + q
    here = c * cells + me
    own = spec_ref.shape[0] // devices
    inputs = spec_ref.shape[1]
    lanes = spec_ref.shape[2]
    beams = weight_ref.shape[2]
    turn_step = pl.program_id(0)
    tiles = inputs // tile

    def ahead(step, sign):
        row = (r + rs + sign * (step % rs)) % rs
        return row * qs + (q + qs + sign * (step // rs)) % qs

    def spectra(step, outgoing, first, count):
        if outgoing:
            chan, cell = (c + step % cs) % cs, ahead(step // cs, 1)
            origin, column = c, me
            slot = here
        else:
            chan, cell = (c + cs - step % cs) % cs, ahead(step // cs, -1)
            origin, column = chan, cell
            slot = chan * cells + cell
        return pltpu.make_async_remote_copy(
            src_ref=spec_ref.at[
                pl.ds((chan * cells + cell) * own, own),
                pl.ds(pl.multiple_of(first, tile), count),
            ],
            dst_ref=x_ref.at[
                :,
                pl.ds(pl.multiple_of(origin * inputs + first, tile), count),
                pl.ds(pl.multiple_of(column * lanes, lanes), lanes),
            ],
            send_sem=send.at[chan * cells + cell],
            recv_sem=recv.at[slot],
            device_id=(chan, cell // qs, cell % qs),
            device_id_type=MESH,
        )

    def weights(step, outgoing):
        if outgoing:
            peer = (q + step) % qs
            slot = q
        else:
            peer = (q + qs - step) % qs
            slot = peer
        return pltpu.make_async_remote_copy(
            src_ref=weight_ref.at[:, pl.ds((r * qs + peer) * own, own)],
            dst_ref=w_ref.at[:, :, pl.ds(pl.multiple_of(slot * beams, beams), beams)],
            send_sem=wsend.at[peer],
            recv_sem=wrecv.at[slot],
            device_id=(c, r, peer),
            device_id_type=MESH,
        )

    keep = pltpu.make_async_copy(
        weight_ref.at[:, pl.ds(me * own, own)],
        w_ref.at[:, :, pl.ds(pl.multiple_of(q * beams, beams), beams)],
        local.at[1],
    )

    @pl.when(turn_step == 0)
    def _():
        def start_weights(step, carry):
            weights(step, True).start()
            return carry

        lax.fori_loop(1, qs, start_weights, 0)
        keep.start()

    @pl.when((turn_step > 0) & (turn_step * tile % group == 0))
    def _():
        def start(step, carry):
            spectra(step, True, turn_step * tile - group, group).start()
            return carry

        lax.fori_loop(1, devices, start, 0)

    @pl.when(turn_step < tiles)
    def _():
        at = pl.ds(pl.multiple_of(turn_step * tile, tile), tile)
        spec_ref[:, at, :] = spectra_tile(
            v_ref, h_ref, flag_ref, coeff_ref, table_ref, filtered_ref, wide_ref
        )

    @pl.when(turn_step == tiles)
    def _():
        stay = pltpu.make_async_copy(
            spec_ref.at[pl.ds(here * own, own)],
            x_ref.at[
                :,
                pl.ds(pl.multiple_of(c * inputs, inputs), inputs),
                pl.ds(pl.multiple_of(me * lanes, lanes), lanes),
            ],
            local.at[0],
        )
        stay.start()

        def finish(step, carry):
            spectra(step, True, 0, inputs).wait_send()
            spectra(step, False, 0, inputs).wait_recv()
            return carry

        def finish_weights(step, carry):
            weights(step, True).wait_send()
            weights(step, False).wait_recv()
            return carry

        lax.fori_loop(1, devices, finish, 0)
        lax.fori_loop(1, qs, finish_weights, 0)
        stay.wait()
        keep.wait()


def turn(voltages, input_flags, channel_order, beam_weights):
    cs, rs, qs = sizes()
    devices = cs * rs * qs
    own = NCH // devices
    _, inputs, samples = voltages.shape
    past = (TAPS - 1) * NCH
    history = passed_along(voltages[:, :, samples - past :], ("row", "col"), 1)
    frames = samples // NCH
    lanes = 2 * frames
    tile = 16
    group = 2 * tile if inputs % (2 * tile) == 0 else tile
    last = inputs // tile - 1
    tables = dft_tables(channel_order, NCH)[:, 0].reshape(NCH, 2 * NCH)
    anywhere = pl.BlockSpec(memory_space=pl.ANY)
    return pl.pallas_call(
        functools.partial(turn_kernel, cs, rs, qs, tile, group),
        grid=(inputs // tile + 1,),
        out_shape=(
            jax.ShapeDtypeStruct((own, inputs * cs, lanes * rs * qs), jnp.bfloat16),
            jax.ShapeDtypeStruct(
                (2, own, beam_weights.shape[2] * qs, beam_weights.shape[3]), beam_weights.dtype
            ),
        ),
        in_specs=[
            pl.BlockSpec((2, tile, samples), lambda i: (0, jnp.minimum(i, last), 0)),
            pl.BlockSpec((2, tile, past), lambda i: (0, jnp.minimum(i, last), 0)),
            pl.BlockSpec((tile, 1), lambda i: (jnp.minimum(i, last), 0)),
            pl.BlockSpec((TAPS, NCH), lambda i: (0, 0)),
            pl.BlockSpec((NCH, 2 * NCH), lambda i: (0, 0)),
            anywhere,
        ],
        out_specs=(anywhere,) * 2,
        scratch_shapes=[
            pltpu.VMEM((2, frames, tile, NCH), jnp.float32),
            pltpu.VMEM((NCH, tile, lanes), jnp.float32),
            pltpu.VMEM((NCH, inputs, lanes), jnp.bfloat16),
            pltpu.SemaphoreType.DMA((devices,)),
            pltpu.SemaphoreType.DMA((devices,)),
            pltpu.SemaphoreType.DMA((qs,)),
            pltpu.SemaphoreType.DMA((qs,)),
            pltpu.SemaphoreType.DMA((2,)),
        ],
        compiler_params=pltpu.CompilerParams(has_side_effects=True, vmem_limit_bytes=60 << 20),
        name="turn",
    )(
        voltages,
        history,
        input_flags.astype(jnp.float32)[:, None],
        prototype(TAPS, NCH),
        tables,
        beam_weights,
    )


def products_kernel(
    rs, qs, frame_count, tile,
    x_ref, w_ref, swap_ref, pool_ref, block_ref, part_ref,
    y_ref, vis_ref, power_ref, send, recv, psend, precv, local,
):
    c, r, q = (lax.axis_index(name) for name in ("chan", "row", "col"))
    cells = rs * qs
    me = r * qs + q
    own, inputs = vis_ref.shape[1], vis_ref.shape[2]
    depth = x_ref.shape[2]
    height, width = block_ref.shape[2], block_ref.shape[3]
    part_height, part_width = part_ref.shape[1], part_ref.shape[2]
    channel = pl.program_id(0)

    def ahead(step, sign):
        row = (r + rs + sign * (step % rs)) % rs
        return row * qs + (q + qs + sign * (step // rs)) % qs

    def vis_at(first, count, row, col):
        return vis_ref.at[
            :,
            pl.ds(first, count),
            pl.ds(pl.multiple_of(row * height, height), height),
            pl.ds(pl.multiple_of(col * width, width), width),
        ]

    def power_at(row, col):
        return power_ref.at[
            pl.ds(pl.multiple_of(col * part_height, part_height), part_height),
            pl.ds(pl.multiple_of(row * part_width, part_width), part_width),
        ]

    def ends(step, outgoing):
        if outgoing:
            cell = ahead(step, 1)
            return cell, me
        cell = ahead(step, -1)
        return cell, cell

    def block(step, outgoing, first, count):
        cell, slot = ends(step, outgoing)
        return pltpu.make_async_remote_copy(
            src_ref=vis_at(first, count, cell // qs, cell % qs),
            dst_ref=block_ref.at[:, pl.ds(slot * own + first, count)],
            send_sem=send.at[cell],
            recv_sem=recv.at[slot],
            device_id=(c, cell // qs, cell % qs),
            device_id_type=MESH,
        )

    def part(step, outgoing):
        cell, slot = ends(step, outgoing)
        return pltpu.make_async_remote_copy(
            src_ref=power_at(cell // qs, cell % qs),
            dst_ref=part_ref.at[slot],
            send_sem=psend.at[cell],
            recv_sem=precv.at[slot],
            device_id=(c, cell // qs, cell % qs),
            device_id_type=MESH,
        )

    @pl.when(channel == 0)
    def _():
        power_ref[...] = jnp.zeros_like(power_ref)

    @pl.when(channel > 0)
    def _():
        def start(step, carry):
            block(step, True, channel - 1, 1).start()
            return carry

        lax.fori_loop(1, cells, start, 0)

    @pl.when(channel < own)
    def _():
        lanes = swap_ref.shape[0]
        across = (((1,), (1,)), ((), ()))

        def rows(step, carry):
            at = pl.ds(pl.multiple_of(step * tile, tile), tile)
            for start in range(0, depth, lanes):
                y_ref[at, start : start + lanes] = jnp.dot(
                    x_ref[0, at, start : start + lanes],
                    swap_ref[...],
                    preferred_element_type=jnp.float32,
                ).astype(jnp.bfloat16)
            re = lax.dot_general(
                x_ref[0, at, :], x_ref[0], across, preferred_element_type=jnp.float32
            )
            vis_ref[0, channel, at, :] = (re / frame_count).astype(vis_ref.dtype)
            im = lax.dot_general(y_ref[at, :], x_ref[0], across, preferred_element_type=jnp.float32)
            vis_ref[1, channel, at, :] = (im / frame_count).astype(vis_ref.dtype)
            return carry

        lax.fori_loop(0, inputs // tile, rows, 0)
        span = 4 * lanes if depth % (4 * lanes) == 0 else lanes

        def columns(step, carry):
            at = pl.ds(pl.multiple_of(step * span, span), span)
            beam = jnp.dot(w_ref[0, 0], x_ref[0, :, at], preferred_element_type=jnp.float32)
            beam = beam - jnp.dot(w_ref[1, 0], y_ref[:, at], preferred_element_type=jnp.float32)
            square = beam * beam
            high = square.astype(jnp.bfloat16)
            low = (square - high.astype(jnp.float32)).astype(jnp.bfloat16)
            pool = pool_ref[at, :]
            return (
                carry
                + jnp.dot(high, pool, preferred_element_type=jnp.float32)
                + jnp.dot(low, pool, preferred_element_type=jnp.float32)
            )

        found = lax.fori_loop(0, depth // span, columns, jnp.zeros(power_ref.shape, jnp.float32))
        lane = lax.broadcasted_iota(jnp.int32, power_ref.shape, 1) % part_width
        power_ref[...] = jnp.where(lane // (part_width // own) == channel, found, power_ref[...])

    @pl.when(channel == own)
    def _():
        stay = pltpu.make_async_copy(
            vis_at(0, own, r, q), block_ref.at[:, pl.ds(me * own, own)], local.at[0]
        )
        keep = pltpu.make_async_copy(power_at(r, q), part_ref.at[me], local.at[1])

        def start(step, carry):
            part(step, True).start()
            return carry

        lax.fori_loop(1, cells, start, 0)
        stay.start()
        keep.start()

        def finish(step, carry):
            block(step, True, 0, own).wait_send()
            block(step, False, 0, own).wait_recv()
            part(step, True).wait_send()
            part(step, False).wait_recv()
            return carry

        lax.fori_loop(1, cells, finish, 0)
        stay.wait()
        keep.wait()


def products(x, weights, frames):
    _, rs, qs = sizes()
    cells = rs * qs
    own, inputs, depth = x.shape
    beams = weights.shape[2]
    bins = depth // (2 * INTEG)
    lanes = 2 * frames
    last = own - 1
    source = jnp.arange(lanes)[:, None]
    goal = jnp.arange(lanes)[None, :]
    swap = jnp.where(source == goal + frames, 1.0, 0.0) - jnp.where(source + frames == goal, 1.0, 0.0)
    at = jnp.arange(depth)
    frame = at // lanes * frames + at % frames
    part = bins // rs
    column = jnp.arange(rs * own * part)
    bin_of = column // (own * part) * part + column % part
    pool = jnp.where(frame[:, None] // INTEG == bin_of[None, :], 1.0 / INTEG, 0.0)
    anywhere = pl.BlockSpec(memory_space=pl.ANY)
    return pl.pallas_call(
        functools.partial(products_kernel, rs, qs, depth // 2, min(inputs, 256)),
        grid=(own + 1,),
        out_shape=(
            jax.ShapeDtypeStruct((2, cells * own, inputs // rs, inputs // qs), jnp.bfloat16),
            jax.ShapeDtypeStruct((cells, beams // qs, own * part), jnp.float32),
        ),
        in_specs=[
            pl.BlockSpec((1, inputs, depth), lambda j: (jnp.minimum(j, last), 0, 0)),
            pl.BlockSpec((2, 1, beams, inputs), lambda j: (0, jnp.minimum(j, last), 0, 0)),
            pl.BlockSpec((lanes, lanes), lambda j: (0, 0)),
            pl.BlockSpec((depth, rs * own * part), lambda j: (0, 0)),
        ],
        out_specs=(anywhere,) * 2,
        scratch_shapes=[
            pltpu.VMEM((inputs, depth), jnp.bfloat16),
            pltpu.VMEM((2, own, inputs, inputs), jnp.bfloat16),
            pltpu.VMEM((beams, rs * own * part), jnp.float32),
        ]
        + [pltpu.SemaphoreType.DMA((cells,))] * 4
        + [pltpu.SemaphoreType.DMA((2,))],
        compiler_params=pltpu.CompilerParams(has_side_effects=True, vmem_limit_bytes=60 << 20),
        name="products",
    )(x, weights, swap.astype(jnp.bfloat16), pool.astype(jnp.bfloat16))


def by_channels(voltages, input_flags, channel_order, beam_weights):
    x, weights = turn(voltages, input_flags, channel_order, beam_weights)
    block, part = products(x, weights, voltages.shape[2] // NCH)
    own = x.shape[0]
    cells, beams, _ = part.shape
    split = part.reshape(cells, beams, own, -1)
    beam_power = jnp.transpose(split, (0, 2, 1, 3)).reshape(cells * own, beams, -1)
    return (block.astype(jnp.float32), beam_power)


def on_device(voltages, input_flags, channel_order, beam_weights):
    cs, rs, qs = sizes()
    lanes = 2 * (voltages.shape[2] // NCH)
    devices = cs * rs * qs
    whole = NCH % devices == 0 and lanes % 128 == 0 and voltages.shape[1] % 16 == 0
    if whole and NCH // devices * (lanes // 2 * qs // INTEG) % 128 == 0:
        plan = by_channels
    else:
        plan = by_panels
    return plan(voltages, input_flags, channel_order, beam_weights)


def solution(mesh):
    placed = (P(None, "chan", ("row", "col")), P("chan"), P(), P(None, "chan", "col", None))
    return jax.shard_map(
        on_device,
        mesh=mesh,
        in_specs=placed,
        out_specs=(P(None, "chan", "row", "col"), P("chan", "col", "row")),
        check_vma=False,
    )
```
